32 devices in a mesh: depth: 4 (over x, core), rows: 8 (over z, y).
Axes of the slice: x: 2, y: 2, z: 4, core: 2. Of those that a mesh axis runs over, the one named last changes fastest.
Arguments:
- volume: bfloat16 [4, 64, 256, 4096], P(None, 'depth', 'rows')
- shear_rows: int32 [64], P('depth'), may hold values from -8 to 8, as said below
- shear_cols: int32 [64], P('depth'), may hold values from -8 to 8, as said below
- warp_cols: int32 [256], replicated, may hold values from -8 to 8, as said below
- warp_rows: int32 [4096], P('depth'), may hold values from -8 to 8, as said below
Outputs:
- final_image: float32 [4, 256, 4096], P(None, 'rows', 'depth')
The draws below stay inside these ranges and needn't reach their ends.
Inputs may be any that keep to these rules, and one draw needn't show every extreme that they name: `shear_rows`: both -8 and 8 occur. `shear_cols`: both -8 and 8 occur. `warp_cols`: both -8 and 8 occur. `warp_rows`: both -8 and 8 occur.
All inputs are finite; a program needn't handle non-finite values.
Results may differ from the reference program's by a relative error of at most 0.0017.
Values may be sent and summed in bfloat16 or wider, within the bound.
A program may use at most 192 MiB of HBM per device.

```python
import jax
import jax.numpy as jnp
from jax import lax

X = 4096
SHIFT = 8
Z = 64
Y = 256


def draw_offsets(key, count):
    first_key, second_key, third_key = jax.random.split(key, 3)
    values = jax.random.randint(first_key, (count,), -SHIFT, SHIFT + 1)
    high_spot = jax.random.randint(second_key, (), 0, count)
    low_spot = (high_spot + 1 + jax.random.randint(third_key, (), 0, count - 1)) % count
    values = values.at[high_spot].set(SHIFT)
    values = values.at[low_spot].set(-SHIFT)
    return values.astype(jnp.int32)


def draw_volume(key, part):
    colour_key, opacity_key = jax.random.split(jax.random.fold_in(key, 11))
    colour = jax.random.uniform(colour_key, (3, Z, Y, X), jnp.float32, 0.0, 2.0)
    opacity = jnp.exp(jax.random.uniform(opacity_key, (1, Z, Y, X), jnp.float32, jnp.log(0.001), jnp.log(0.06)))
    return jnp.concatenate([colour, opacity], 0).astype(jnp.bfloat16)


def draw_shear_rows(key, part):
    return draw_offsets(jax.random.fold_in(key, 21), Z)


def draw_shear_cols(key, part):
    return draw_offsets(jax.random.fold_in(key, 22), Z)


def draw_warp_cols(key, part):
    return draw_offsets(jax.random.fold_in(key, 23), Y)


def draw_warp_rows(key, part):
    return draw_offsets(jax.random.fold_in(key, 24), X)


def setup_inputs(seed: int = 0) -> dict:
    arg_keys = jax.random.split(jax.random.key(seed), 6)
    volume = draw_volume(jax.random.fold_in(arg_keys[5], 71), 0)
    shear_rows = draw_shear_rows(jax.random.fold_in(arg_keys[5], 71), 0)
    shear_cols = draw_shear_cols(jax.random.fold_in(arg_keys[5], 71), 0)
    warp_cols = draw_warp_cols(jax.random.fold_in(arg_keys[5], 71), 0)
    warp_rows = draw_warp_rows(jax.random.fold_in(arg_keys[5], 71), 0)
    return {"volume": volume, "shear_rows": shear_rows, "shear_cols": shear_cols, "warp_cols": warp_cols, "warp_rows": warp_rows}


def weight_of(offset):
    return jnp.where(offset == 0, 0.5, jnp.where(jnp.abs(offset) == 1, 0.25, 0.0)).astype(jnp.float32)


def over_front(front_part, back_part):
    return front_part + (1.0 - front_part[3:4]) * back_part


def premultiply(slab):
    opacity = slab[3:4]
    return jnp.concatenate([slab[:3] * opacity, opacity], 0)


def shear_slice(extended, row_shift, col_shift, band_rows, band_cols, rim_width):
    band_sum = jnp.zeros((4, band_rows, band_cols + 2 * rim_width), jnp.float32)
    for offset, factor in ((-1, 0.25), (0, 0.5), (1, 0.25)):
        start = (rim_width + row_shift + offset).astype(jnp.int32)
        band_sum = band_sum + factor * lax.dynamic_slice_in_dim(extended, start, band_rows, 1)
    sheared = jnp.zeros((4, band_rows, band_cols), jnp.float32)
    for offset, factor in ((-1, 0.25), (0, 0.5), (1, 0.25)):
        start = (rim_width + col_shift + offset).astype(jnp.int32)
        sheared = sheared + factor * lax.dynamic_slice_in_dim(band_sum, start, band_cols, 2)
    return sheared


def shift_columns(picture, shifts, band_cols, rim_width):
    result = jnp.zeros((4, picture.shape[1], band_cols), jnp.float32)
    for offset in range(-rim_width, rim_width + 1):
        kernel_col = weight_of(offset - shifts)[None, :, None]
        result = result + kernel_col * picture[:, :, rim_width + offset:rim_width + offset + band_cols]
    return result


def shift_rows(picture, shifts, band_rows, rim_width):
    result = jnp.zeros((4, band_rows, picture.shape[2]), jnp.float32)
    for offset in range(-rim_width, rim_width + 1):
        kernel_row = weight_of(offset - shifts)[None, None, :]
        result = result + kernel_row * picture[:, rim_width + offset:rim_width + offset + band_rows, :]
    return result


def reference(volume, shear_rows, shear_cols, warp_cols, warp_rows):
    rim_width = SHIFT + 1
    slices_first = jnp.moveaxis(volume, 1, 0)

    def add_slice(accumulated, pieces_in):
        slice_now, row_shift, col_shift = pieces_in
        extended = jnp.pad(premultiply(slice_now.astype(jnp.float32)), ((0, 0), (rim_width, rim_width), (rim_width, rim_width)))
        return over_front(accumulated, shear_slice(extended, row_shift, col_shift, Y, X, rim_width)), None

    start_image = jnp.zeros((4, Y, X), jnp.float32)
    intermediate, _ = lax.scan(add_slice, start_image, (slices_first, shear_rows, shear_cols))
    padded_cols = jnp.pad(intermediate, ((0, 0), (0, 0), (rim_width, rim_width)))
    across = shift_columns(padded_cols, warp_cols, X, rim_width)
    padded_rows = jnp.pad(across, ((0, 0), (rim_width, rim_width), (0, 0)))
    return shift_rows(padded_rows, warp_rows, Y, rim_width)
```

```python
import functools

import jax
import jax.numpy as jnp
from jax import lax
from jax.experimental import pallas as pl
from jax.experimental.pallas import tpu as pltpu
from jax.sharding import PartitionSpec as P

SHIFT = 8
RIM = SHIFT + 1
GROUP = 16
PAD = 128
BF = jnp.bfloat16
F32 = jnp.float32


def weight_of(offset):
    return jnp.where(offset == 0, 0.5, jnp.where(jnp.abs(offset) == 1, 0.25, 0.0)).astype(F32)


def iota(shape, dim):
    return lax.broadcasted_iota(jnp.int32, shape, dim)


def pack_kernel(vol_ref, pick_up_ref, pick_dn_ref, up_ref, dn_ref):
    _, slab, rows, cols = vol_ref.shape
    groups = up_ref.shape[0]
    for pick_ref, out_ref, first in ((pick_up_ref, up_ref, 0), (pick_dn_ref, dn_ref, rows - GROUP)):
        pick = pick_ref[...]
        opacity = None
        for c in (3, 2, 1, 0):
            source = vol_ref[c, :, first : first + GROUP, :].reshape(slab * GROUP, cols)
            got = jnp.dot(pick, source, preferred_element_type=F32)
            if c == 3:
                opacity = got
            else:
                got = got * opacity
            out_ref[:, c, :, :] = got.astype(BF).reshape(groups, GROUP, cols)


def pack(volume, pick_up, pick_dn):
    channels, slab, rows, cols = volume.shape
    count = pick_up.shape[0]
    groups = count // GROUP
    block = 512
    out_spec = pl.BlockSpec((groups, channels, GROUP, block), lambda i: (0, 0, 0, i))
    pick_spec = pl.BlockSpec(pick_up.shape, lambda i: (0, 0))
    shape = jax.ShapeDtypeStruct((groups, channels, GROUP, cols), BF)
    return pl.pallas_call(
        pack_kernel,
        grid=(cols // block,),
        in_specs=[
            pl.BlockSpec((channels, slab, rows, block), lambda i: (0, 0, 0, i)),
            pick_spec,
            pick_spec,
        ],
        out_specs=[out_spec, out_spec],
        out_shape=[shape, shape],
        name="pack_rows",
    )(volume, pick_up, pick_dn)


def slab_kernel(row_s, col_s, off_up, off_dn, vol_ref, up_ref, dn_ref, out_ref, band_ref, acc_ref):
    k = pl.program_id(0)
    channels, rows, cols = vol_ref.shape
    groups = up_ref.shape[0]
    tiles, _, _, wide = out_ref.shape
    tile = wide - 2 * PAD

    @pl.when(k == 0)
    def _():
        acc_ref[...] = jnp.zeros_like(acc_ref)
        band_ref[...] = jnp.zeros_like(band_ref)

    s = row_s[k]
    t = col_s[k]
    ou = off_up[k]
    od = off_dn[k]
    gu = jnp.minimum(ou // GROUP, groups - 2)
    gd = jnp.minimum(od // GROUP, groups - 2)
    y = iota((rows, rows), 0)
    r = iota((rows, rows), 1)
    w_own = weight_of(r - y - s).astype(BF)
    window = (rows, 2 * GROUP)
    y = iota(window, 0)
    d = gu * GROUP + iota(window, 1) - ou
    w_up = jnp.where(d >= 0, weight_of(rows + d - y - s), 0.0).astype(BF)
    count = jnp.maximum(0, 1 - s)
    d = gd * GROUP + iota(window, 1) - od - count
    w_dn = jnp.where(d < 0, weight_of(d - y - s), 0.0).astype(BF)
    w_all = jnp.concatenate([w_own, w_up, w_dn], 1)

    chunk = 512

    @pl.loop(0, cols // chunk)
    def _(j):
        at = pl.multiple_of(j * chunk, chunk)
        here = pl.ds(at, chunk)
        opacity = vol_ref[channels - 1, :, here]
        for c in range(channels):
            own = opacity if c == channels - 1 else vol_ref[c, :, here] * opacity
            data = jnp.concatenate(
                [
                    own,
                    up_ref[gu, c, :, here],
                    up_ref[gu + 1, c, :, here],
                    dn_ref[gd, c, :, here],
                    dn_ref[gd + 1, c, :, here],
                ],
                0,
            )
            band = jnp.dot(w_all, data, preferred_element_type=F32)
            band_ref[c * rows : (c + 1) * rows, pl.ds(at + PAD, chunk)] = band.astype(BF)

    block = 256
    shape = (block + 2 * PAD, block)
    w_col = weight_of(iota(shape, 0) - PAD - iota(shape, 1) - t).astype(BF)

    @pl.loop(0, cols // block)
    def _(j):
        at = pl.multiple_of(j * block, block)
        here = pl.ds(at, block)
        sheared = jnp.dot(
            band_ref[:, pl.ds(at, block + 2 * PAD)], w_col, preferred_element_type=F32
        )
        clear = 1.0 - acc_ref[channels - 1, :, here]
        for c in range(channels):
            acc_ref[c, :, here] += clear * sheared[c * rows : (c + 1) * rows, :]

    @pl.when(k == pl.num_programs(0) - 1)
    def _():
        edge = jnp.zeros((channels, rows, PAD), BF)
        for i in range(tiles):
            low = i * tile - PAD
            high = (i + 1) * tile + PAD
            if i == 0:
                out_ref[i, :, :, :PAD] = edge
            else:
                out_ref[i, :, :, :PAD] = acc_ref[:, :, low : low + PAD].astype(BF)
            out_ref[i, :, :, PAD : PAD + tile] = acc_ref[:, :, i * tile : (i + 1) * tile].astype(BF)
            if i == tiles - 1:
                out_ref[i, :, :, PAD + tile :] = edge
            else:
                out_ref[i, :, :, PAD + tile :] = acc_ref[:, :, high - PAD : high].astype(BF)


def slab_image(volume, up, dn, row_s, col_s, off_up, off_dn, tiles):
    channels, slab, rows, cols = volume.shape
    wide = cols // tiles + 2 * PAD
    halo = pl.BlockSpec(up.shape, lambda k, *_: (0, 0, 0, 0))
    return pl.pallas_call(
        slab_kernel,
        grid_spec=pltpu.PrefetchScalarGridSpec(
            num_scalar_prefetch=4,
            grid=(slab,),
            in_specs=[
                pl.BlockSpec((channels, None, rows, cols), lambda k, *_: (0, k, 0, 0)),
                halo,
                halo,
            ],
            out_specs=pl.BlockSpec((tiles, channels, rows, wide), lambda k, *_: (0, 0, 0, 0)),
            scratch_shapes=[
                pltpu.VMEM((channels * rows, cols + 2 * PAD), BF),
                pltpu.VMEM((channels, rows, cols), F32),
            ],
        ),
        out_shape=jax.ShapeDtypeStruct((tiles, channels, rows, wide), BF),
        compiler_params=pltpu.CompilerParams(vmem_limit_bytes=56 * 2**20),
        name="slab_image",
    )(row_s, col_s, off_up, off_dn, volume, up, dn)


def across_kernel(me_ref, shift_ref, *refs):
    part_refs = refs[:-3]
    out_ref, low_ref, high_ref = refs[-3:]
    count = len(part_refs)
    _, channels, rows, wide = (1,) + part_refs[0].shape
    tile = wide - 2 * PAD
    me = me_ref[0]

    def gather(position):
        result = part_refs[0][...].astype(F32)
        for m in range(1, count):
            result = jnp.where((position ^ me) == m, part_refs[m][...].astype(F32), result)
        return result

    image = gather(0)
    for position in range(1, count):
        image = image + (1.0 - image[channels - 1 : channels]) * gather(position)
    shifts = shift_ref[...]
    for c in range(channels):
        flat = image[c]
        spread = 0.5 * flat + 0.25 * (pltpu.roll(flat, 1, 1) + pltpu.roll(flat, wide - 1, 1))
        moved = jnp.zeros_like(flat)
        for v in range(-SHIFT, SHIFT + 1):
            rolled = spread if v == 0 else pltpu.roll(spread, (-v) % wide, 1)
            moved = jnp.where(shifts == v, rolled, moved)
        across = moved[:, PAD : PAD + tile]
        out_ref[c] = across
        low_ref[c] = across[:GROUP].astype(BF)
        high_ref[c] = across[rows - GROUP :].astype(BF)


def across_image(parts, me, shifts):
    channels, rows, wide = parts[0].shape
    tile = wide - 2 * PAD
    vmem = pl.BlockSpec(memory_space=pltpu.VMEM)
    half = jax.ShapeDtypeStruct((channels, GROUP, tile), BF)
    return pl.pallas_call(
        across_kernel,
        in_specs=[pl.BlockSpec(memory_space=pltpu.SMEM), vmem] + [vmem] * len(parts),
        out_specs=[vmem] * 3,
        out_shape=[jax.ShapeDtypeStruct((channels, rows, tile), F32), half, half],
        name="across_image",
    )(me, shifts, *parts)


def final_kernel(shift_ref, mid_ref, low_ref, high_ref, out_ref, ext_ref):
    channels, rows, tile = mid_ref.shape
    shifts = shift_ref[...]
    for c in range(channels):
        ext_ref[:GROUP] = low_ref[c].astype(F32)
        ext_ref[GROUP : GROUP + rows] = mid_ref[c]
        ext_ref[GROUP + rows :] = high_ref[c].astype(F32)
        moved = jnp.zeros((rows + 2, tile), F32)
        for v in range(-SHIFT, SHIFT + 1):
            start = GROUP + v - 1
            moved = jnp.where(shifts == v, ext_ref[start : start + rows + 2], moved)
        out_ref[c] = 0.5 * moved[1 : rows + 1] + 0.25 * (moved[:rows] + moved[2 : rows + 2])


def final_rows(mid, low, high, shifts):
    channels, rows, tile = mid.shape
    block = 256
    return pl.pallas_call(
        final_kernel,
        grid=(tile // block,),
        in_specs=[
            pl.BlockSpec((1, block), lambda i: (0, i)),
            pl.BlockSpec((channels, rows, block), lambda i: (0, 0, i)),
            pl.BlockSpec((channels, GROUP, block), lambda i: (0, 0, i)),
            pl.BlockSpec((channels, GROUP, block), lambda i: (0, 0, i)),
        ],
        out_specs=pl.BlockSpec((channels, rows, block), lambda i: (0, 0, i)),
        out_shape=jax.ShapeDtypeStruct((channels, rows, tile), F32),
        scratch_shapes=[pltpu.VMEM((rows + 2 * GROUP, block), F32)],
        name="final_rows",
    )(shifts, mid, low, high)


def neighbours(axis):
    count = lax.axis_size(axis)
    forward = [(i, i + 1) for i in range(count - 1)]
    return forward, [(b, a) for a, b in forward]


def swapped(value, axis, mask):
    pairs = [(source, source ^ mask) for source in range(lax.axis_size(axis))]
    return lax.ppermute(value, axis, pairs)


def per_device(volume, shear_rows, shear_cols, warp_cols, warp_rows):
    channels, slab, rows, cols = volume.shape
    depth = lax.axis_size("depth")
    me = lax.axis_index("depth")
    groups = -(-slab * RIM // GROUP)
    forward, backward = neighbours("rows")

    n_up = jnp.maximum(0, shear_rows + 1)
    n_dn = jnp.maximum(0, 1 - shear_rows)
    end_up = jnp.cumsum(n_up)
    end_dn = jnp.cumsum(n_dn)
    off_up = end_up - n_up
    off_dn = end_dn - n_dn
    need = jnp.maximum(end_up[-1], end_dn[-1]).astype(jnp.int32)
    step = 1
    while step < depth:
        need = jnp.maximum(need, swapped(need, "depth", step))
        step *= 2
    row = jnp.arange(GROUP, dtype=jnp.int32)
    at_up = jnp.where(row[None] < n_up[:, None], off_up[:, None] + row[None], -1).reshape(-1)
    back = row[None] - (GROUP - n_dn[:, None])
    at_dn = jnp.where(back >= 0, off_dn[:, None] + back, -1).reshape(-1)
    slot = jnp.arange(groups * GROUP, dtype=jnp.int32)[:, None]
    pick_up = (slot == at_up[None]).astype(BF)
    pick_dn = (slot == at_dn[None]).astype(BF)
    send_up, send_dn = pack(volume, pick_up, pick_dn)

    def exchange(count):
        def run(a, b):
            got_up = lax.ppermute(a[:count], "rows", backward)
            got_dn = lax.ppermute(b[:count], "rows", forward)
            rest = ((0, groups - count), (0, 0), (0, 0), (0, 0))
            return jnp.pad(got_up, rest), jnp.pad(got_dn, rest)

        return run

    which = jnp.clip((need + GROUP - 1) // GROUP - 1, 0, groups - 1)
    up, dn = lax.switch(which, [exchange(c + 1) for c in range(groups)], send_up, send_dn)

    tiles = slab_image(volume, up, dn, shear_rows, shear_cols, off_up, off_dn, depth)
    parts = []
    for m in range(depth):
        part = lax.dynamic_index_in_dim(tiles, me ^ m, 0, keepdims=False)
        parts.append(part if m == 0 else swapped(part, "depth", m))
    row_start = lax.axis_index("rows") * rows
    row_shifts = lax.dynamic_slice_in_dim(warp_cols, row_start, rows, 0)
    mid, low, high = across_image(parts, me.reshape(1), row_shifts.reshape(rows, 1))
    below = lax.ppermute(high, "rows", forward)
    above = lax.ppermute(low, "rows", backward)
    return final_rows(mid, below, above, warp_rows.reshape(1, -1))


def solution(mesh):
    return jax.shard_map(
        per_device,
        mesh=mesh,
        in_specs=(P(None, "depth", "rows", None), P("depth"), P("depth"), P(), P("depth")),
        out_specs=P(None, "rows", "depth"),
        check_vma=False,
    )
```

```python
import functools

import jax
import jax.numpy as jnp
from jax import lax
from jax.experimental import pallas as pl
from jax.experimental.pallas import tpu as pltpu
from jax.sharding import PartitionSpec as P

SHIFT = 8
RIM = SHIFT + 1
GROUP = 16
PAD = 128
BF = jnp.bfloat16
F32 = jnp.float32


def weight_of(offset):
    return jnp.where(offset == 0, 0.5, jnp.where(jnp.abs(offset) == 1, 0.25, 0.0)).astype(F32)


def iota(shape, dim):
    return lax.broadcasted_iota(jnp.int32, shape, dim)


def pack_kernel(vol_ref, pick_up_ref, pick_dn_ref, up_ref, dn_ref):
    _, slab, rows, cols = vol_ref.shape
    groups = up_ref.shape[0]
    for pick_ref, out_ref, first in ((pick_up_ref, up_ref, 0), (pick_dn_ref, dn_ref, rows - GROUP)):
        pick = pick_ref[...]
        opacity = None
        for c in (3, 2, 1, 0):
            source = vol_ref[c, :, first : first + GROUP, :].reshape(slab * GROUP, cols)
            got = jnp.dot(pick, source, preferred_element_type=F32)
            if c == 3:
                opacity = got
            else:
                got = got * opacity
            out_ref[:, c, :, :] = got.astype(BF).reshape(groups, GROUP, cols)


def pack(volume, pick_up, pick_dn):
    channels, slab, rows, cols = volume.shape
    count = pick_up.shape[0]
    groups = count // GROUP
    block = 512
    out_spec = pl.BlockSpec((groups, channels, GROUP, block), lambda i: (0, 0, 0, i))
    pick_spec = pl.BlockSpec(pick_up.shape, lambda i: (0, 0))
    shape = jax.ShapeDtypeStruct((groups, channels, GROUP, cols), BF)
    return pl.pallas_call(
        pack_kernel,
        grid=(cols // block,),
        in_specs=[
            pl.BlockSpec((channels, slab, rows, block), lambda i: (0, 0, 0, i)),
            pick_spec,
            pick_spec,
        ],
        out_specs=[out_spec, out_spec],
        out_shape=[shape, shape],
        name="pack_rows",
    )(volume, pick_up, pick_dn)


def slab_kernel(
    cuts, bounds, first, last, row_s, col_s, off_up, off_dn, vol_ref, *refs
):
    parts = len(cuts)
    up_refs, dn_refs = refs[:parts], refs[parts : 2 * parts]
    refs = refs[2 * parts :]
    acc_in = None
    if not first:
        acc_in, refs = refs[0], refs[1:]
    out_ref, held_ref, band_ref, acc_ref, sems = refs
    step = pl.program_id(0)
    channels, rows, cols = vol_ref.shape
    k = bounds[0] + step

    @pl.when(step == 0)
    def _():
        copies = []
        start = 0
        for p in range(parts):
            size = cuts[p]
            for d, source in enumerate((up_refs[p], dn_refs[p])):
                target = held_ref.at[pl.ds(d * sum(cuts) + start, size)]
                copies.append(pltpu.make_async_copy(source, target, sems.at[2 * p + d]))
            start += size
        if not first:
            copies.append(pltpu.make_async_copy(acc_in, acc_ref, sems.at[2 * parts]))
        for copy in copies:
            copy.start()
        if first:
            acc_ref[...] = jnp.zeros_like(acc_ref)
        band_ref[...] = jnp.zeros_like(band_ref)
        for copy in copies:
            copy.wait()

    @pl.when(k < bounds[1])
    def _():
        s = row_s[k]
        t = col_s[k]
        chunk = 512
        total = sum(cuts)
        ou = off_up[k]
        od = off_dn[k]
        count = jnp.maximum(0, 1 - s)
        gu = jnp.minimum(ou // GROUP, total - jnp.where(s > 0, 2, 1))
        gd = jnp.minimum(od // GROUP, total - jnp.where(s < 0, 2, 1))
        row_up = rows + gu * GROUP - ou
        row_dn = gd * GROUP - od - count
        g0 = jnp.where(s >= 0, gu, total + gd)
        g1 = jnp.where(s > 0, gu + 1, total + gd + jnp.where(s < 0, 1, 0))
        y = iota((rows, rows), 0)
        r = iota((rows, rows), 1)
        w_own = weight_of(r - y - s)
        y = iota((rows, GROUP), 0)
        q = iota((rows, GROUP), 1)
        r = q + jnp.where(s >= 0, row_up, row_dn)
        kept = jnp.where(s >= 0, r - rows, -1 - r) >= 0
        w_0 = jnp.where(kept, weight_of(r - y - s), 0.0)
        r = q + jnp.where(s > 0, row_up + GROUP, row_dn + jnp.where(s < 0, GROUP, 0))
        kept = jnp.where(s > 0, r - rows, -1 - r) >= 0
        w_1 = jnp.where(kept, weight_of(r - y - s), 0.0)
        w_all = jnp.concatenate([w_own, w_0, w_1], 1).astype(BF)

        @pl.loop(0, cols // chunk)
        def _(j):
            at = pl.multiple_of(j * chunk, chunk)
            here = pl.ds(at, chunk)
            opacity = vol_ref[channels - 1, :, here]
            for c in range(channels):
                own = opacity if c == channels - 1 else vol_ref[c, :, here] * opacity
                data = jnp.concatenate([own, held_ref[g0, c, :, here], held_ref[g1, c, :, here]], 0)
                band = jnp.dot(w_all, data, preferred_element_type=F32)
                band_ref[c * rows : (c + 1) * rows, pl.ds(at + PAD, chunk)] = band.astype(BF)

        block = 256
        shape = (block + 2 * PAD, block)
        w_col = weight_of(iota(shape, 0) - PAD - iota(shape, 1) - t).astype(BF)

        @pl.loop(0, cols // block)
        def _(j):
            at = pl.multiple_of(j * block, block)
            here = pl.ds(at, block)
            sheared = jnp.dot(
                band_ref[:, pl.ds(at, block + 2 * PAD)], w_col, preferred_element_type=F32
            )
            clear = 1.0 - acc_ref[channels - 1, :, here]
            for c in range(channels):
                acc_ref[c, :, here] += clear * sheared[c * rows : (c + 1) * rows, :]

    @pl.when(step == pl.num_programs(0) - 1)
    def _():
        if not last:
            copy = pltpu.make_async_copy(acc_ref, out_ref, sems.at[2 * parts])
            copy.start()
            copy.wait()
            return
        tiles, _, _, wide = out_ref.shape
        tile = wide - 2 * PAD
        edge = jnp.zeros((channels, rows, PAD), BF)
        for i in range(tiles):
            low = i * tile - PAD
            high = (i + 1) * tile + PAD
            if i == 0:
                out_ref[i, :, :, :PAD] = edge
            else:
                out_ref[i, :, :, :PAD] = acc_ref[:, :, low : low + PAD].astype(BF)
            out_ref[i, :, :, PAD : PAD + tile] = acc_ref[:, :, i * tile : (i + 1) * tile].astype(BF)
            if i == tiles - 1:
                out_ref[i, :, :, PAD + tile :] = edge
            else:
                out_ref[i, :, :, PAD + tile :] = acc_ref[:, :, high - PAD : high].astype(BF)


def slab_stage(volume, ups, dns, carry, bounds, scalars, cuts, tiles, last):
    channels, slab, rows, cols = volume.shape
    wide = cols // tiles + 2 * PAD
    parts = len(cuts)
    first = carry is None
    hbm = pl.BlockSpec(memory_space=pl.ANY)
    held = pltpu.VMEM((2 * sum(cuts), channels, GROUP, cols), BF)

    def slice_at(i, bounds_ref, *_):
        return 0, jnp.clip(bounds_ref[0] + i, 0, jnp.maximum(bounds_ref[1] - 1, 0)), 0, 0

    if last:
        out_spec = pl.BlockSpec((tiles, channels, rows, wide), lambda i, *_: (0, 0, 0, 0))
        out_shape = jax.ShapeDtypeStruct((tiles, channels, rows, wide), BF)
    else:
        out_spec = hbm
        out_shape = jax.ShapeDtypeStruct((channels, rows, cols), F32)
    return pl.pallas_call(
        functools.partial(slab_kernel_entry, cuts, first, last),
        grid_spec=pltpu.PrefetchScalarGridSpec(
            num_scalar_prefetch=5,
            grid=(slab,),
            in_specs=[pl.BlockSpec((channels, None, rows, cols), slice_at)]
            + [hbm] * (2 * parts + (0 if first else 1)),
            out_specs=out_spec,
            scratch_shapes=[
                held,
                pltpu.VMEM((channels * rows, cols + 2 * PAD), BF),
                pltpu.VMEM((channels, rows, cols), F32),
                pltpu.SemaphoreType.DMA((2 * parts + 1,)),
            ],
        ),
        out_shape=out_shape,
        compiler_params=pltpu.CompilerParams(vmem_limit_bytes=56 * 2**20),
        cost_estimate=pl.CostEstimate(
            flops=2 * 10**10, bytes_accessed=10**8, transcendentals=0
        ),
        name="slab_stage",
    )(bounds, *scalars, volume, *ups, *dns, *([] if first else [carry]))


def slab_kernel_entry(cuts, first, last, bounds, *refs):
    slab_kernel(cuts, bounds, first, last, *refs)


def cuts_of(count):
    if count < 4:
        return [count]
    small = count // 3
    big = count - 2 * small
    return [big, small, small] if count % 3 != 2 else [small + 1, small + 1, small]


def across_kernel(me_ref, shift_ref, *refs):
    part_refs = refs[:-3]
    out_ref, low_ref, high_ref = refs[-3:]
    count = len(part_refs)
    _, channels, rows, wide = (1,) + part_refs[0].shape
    tile = wide - 2 * PAD
    me = me_ref[0]

    def gather(position):
        result = part_refs[0][...].astype(F32)
        for m in range(1, count):
            result = jnp.where((position ^ me) == m, part_refs[m][...].astype(F32), result)
        return result

    image = gather(0)
    for position in range(1, count):
        image = image + (1.0 - image[channels - 1 : channels]) * gather(position)
    shifts = shift_ref[...]
    for c in range(channels):
        flat = image[c]
        spread = 0.5 * flat + 0.25 * (pltpu.roll(flat, 1, 1) + pltpu.roll(flat, wide - 1, 1))
        moved = jnp.zeros_like(flat)
        for v in range(-SHIFT, SHIFT + 1):
            rolled = spread if v == 0 else pltpu.roll(spread, (-v) % wide, 1)
            moved = jnp.where(shifts == v, rolled, moved)
        across = moved[:, PAD : PAD + tile]
        out_ref[c] = across
        low_ref[c] = across[:GROUP].astype(BF)
        high_ref[c] = across[rows - GROUP :].astype(BF)


def across_image(parts, me, shifts):
    channels, rows, wide = parts[0].shape
    tile = wide - 2 * PAD
    vmem = pl.BlockSpec(memory_space=pltpu.VMEM)
    half = jax.ShapeDtypeStruct((channels, GROUP, tile), BF)
    return pl.pallas_call(
        across_kernel,
        in_specs=[pl.BlockSpec(memory_space=pltpu.SMEM), vmem] + [vmem] * len(parts),
        out_specs=[vmem] * 3,
        out_shape=[jax.ShapeDtypeStruct((channels, rows, tile), F32), half, half],
        name="across_image",
    )(me, shifts, *parts)


def final_kernel(shift_ref, mid_ref, low_ref, high_ref, out_ref, ext_ref):
    channels, rows, tile = mid_ref.shape
    shifts = shift_ref[...]
    for c in range(channels):
        ext_ref[:GROUP] = low_ref[c].astype(F32)
        ext_ref[GROUP : GROUP + rows] = mid_ref[c]
        ext_ref[GROUP + rows :] = high_ref[c].astype(F32)
        moved = jnp.zeros((rows + 2, tile), F32)
        for v in range(-SHIFT, SHIFT + 1):
            start = GROUP + v - 1
            moved = jnp.where(shifts == v, ext_ref[start : start + rows + 2], moved)
        out_ref[c] = 0.5 * moved[1 : rows + 1] + 0.25 * (moved[:rows] + moved[2 : rows + 2])


def final_rows(mid, low, high, shifts):
    channels, rows, tile = mid.shape
    block = 256
    return pl.pallas_call(
        final_kernel,
        grid=(tile // block,),
        in_specs=[
            pl.BlockSpec((1, block), lambda i: (0, i)),
            pl.BlockSpec((channels, rows, block), lambda i: (0, 0, i)),
            pl.BlockSpec((channels, GROUP, block), lambda i: (0, 0, i)),
            pl.BlockSpec((channels, GROUP, block), lambda i: (0, 0, i)),
        ],
        out_specs=pl.BlockSpec((channels, rows, block), lambda i: (0, 0, i)),
        out_shape=jax.ShapeDtypeStruct((channels, rows, tile), F32),
        scratch_shapes=[pltpu.VMEM((rows + 2 * GROUP, block), F32)],
        name="final_rows",
    )(shifts, mid, low, high)


def neighbours(axis):
    count = lax.axis_size(axis)
    forward = [(i, i + 1) for i in range(count - 1)]
    return forward, [(b, a) for a, b in forward]


def swapped(value, axis, mask):
    pairs = [(source, source ^ mask) for source in range(lax.axis_size(axis))]
    return lax.ppermute(value, axis, pairs)


def per_device(volume, shear_rows, shear_cols, warp_cols, warp_rows):
    channels, slab, rows, cols = volume.shape
    depth = lax.axis_size("depth")
    me = lax.axis_index("depth")
    groups = -(-slab * RIM // GROUP)
    forward, backward = neighbours("rows")

    n_up = jnp.maximum(0, shear_rows + 1)
    n_dn = jnp.maximum(0, 1 - shear_rows)
    end_up = jnp.cumsum(n_up)
    end_dn = jnp.cumsum(n_dn)
    off_up = end_up - n_up
    off_dn = end_dn - n_dn
    need = jnp.maximum(end_up[-1], end_dn[-1]).astype(jnp.int32)
    step = 1
    while step < depth:
        need = jnp.maximum(need, swapped(need, "depth", step))
        step *= 2
    row = jnp.arange(GROUP, dtype=jnp.int32)
    at_up = jnp.where(row[None] < n_up[:, None], off_up[:, None] + row[None], -1).reshape(-1)
    back = row[None] - (GROUP - n_dn[:, None])
    at_dn = jnp.where(back >= 0, off_dn[:, None] + back, -1).reshape(-1)
    slot = jnp.arange(groups * GROUP, dtype=jnp.int32)[:, None]
    pick_up = (slot == at_up[None]).astype(BF)
    pick_dn = (slot == at_dn[None]).astype(BF)
    send_up, send_dn = pack(volume, pick_up, pick_dn)

    scalars = (shear_rows, shear_cols, off_up, off_dn)

    def render(count):
        cuts = cuts_of(count)

        def run(a, b):
            ups, dns, carry, start, done = [], [], None, 0, jnp.int32(0)
            for p, size in enumerate(cuts):
                ups.append(lax.ppermute(a[start : start + size], "rows", backward))
                dns.append(lax.ppermute(b[start : start + size], "rows", forward))
                start += size
            start = 0
            for p, size in enumerate(cuts):
                start += size
                last = p == len(cuts) - 1
                if last:
                    until = jnp.int32(slab)
                else:
                    ready = (end_up <= start * GROUP) & (end_dn <= start * GROUP)
                    until = jnp.sum(ready.astype(jnp.int32))
                bounds = jnp.stack([done, until])
                carry = slab_stage(
                    volume, ups[: p + 1], dns[: p + 1], carry, bounds, scalars,
                    cuts[: p + 1], depth, last,
                )
                done = until
            return carry

        return run

    sizes = sorted(set(range(max(2, groups // 2), groups // 2 + 3)) | {groups})
    which = sum((need > size * GROUP).astype(jnp.int32) for size in sizes[:-1])
    tiles = lax.switch(which, [render(size) for size in sizes], send_up, send_dn)
    parts = []
    for m in range(depth):
        part = lax.dynamic_index_in_dim(tiles, me ^ m, 0, keepdims=False)
        parts.append(part if m == 0 else swapped(part, "depth", m))
    row_start = lax.axis_index("rows") * rows
    row_shifts = lax.dynamic_slice_in_dim(warp_cols, row_start, rows, 0)
    mid, low, high = across_image(parts, me.reshape(1), row_shifts.reshape(rows, 1))
    below = lax.ppermute(high, "rows", forward)
    above = lax.ppermute(low, "rows", backward)
    return final_rows(mid, below, above, warp_rows.reshape(1, -1))


def solution(mesh):
    return jax.shard_map(
        per_device,
        mesh=mesh,
        in_specs=(P(None, "depth", "rows", None), P("depth"), P("depth"), P(), P("depth")),
        out_specs=P(None, "rows", "depth"),
        check_vma=False,
    )
```

```python
import functools

import jax
import jax.numpy as jnp
from jax import lax
from jax.experimental import pallas as pl
from jax.experimental.pallas import tpu as pltpu
from jax.sharding import PartitionSpec as P

SHIFT = 8
RIM = SHIFT + 1
GROUP = 16
PAD = 128
BF = jnp.bfloat16
F32 = jnp.float32


def weight_of(offset):
    return jnp.where(offset == 0, 0.5, jnp.where(jnp.abs(offset) == 1, 0.25, 0.0)).astype(F32)


def iota(shape, dim):
    return lax.broadcasted_iota(jnp.int32, shape, dim)


def pack_kernel(vol_ref, pick_up_ref, pick_dn_ref, up_ref, dn_ref):
    _, slab, rows, cols = vol_ref.shape
    groups = up_ref.shape[0]
    for pick_ref, out_ref, first in ((pick_up_ref, up_ref, 0), (pick_dn_ref, dn_ref, rows - GROUP)):
        pick = pick_ref[...]
        opacity = None
        for c in (3, 2, 1, 0):
            source = vol_ref[c, :, first : first + GROUP, :].reshape(slab * GROUP, cols)
            got = jnp.dot(pick, source, preferred_element_type=F32)
            if c == 3:
                opacity = got
            else:
                got = got * opacity
            out_ref[:, c, :, :] = got.astype(BF).reshape(groups, GROUP, cols)


def pack(volume, pick_up, pick_dn):
    channels, slab, rows, cols = volume.shape
    count = pick_up.shape[0]
    groups = count // GROUP
    block = 512
    out_spec = pl.BlockSpec((groups, channels, GROUP, block), lambda i: (0, 0, 0, i))
    pick_spec = pl.BlockSpec(pick_up.shape, lambda i: (0, 0))
    shape = jax.ShapeDtypeStruct((groups, channels, GROUP, cols), BF)
    return pl.pallas_call(
        pack_kernel,
        grid=(cols // block,),
        in_specs=[
            pl.BlockSpec((channels, slab, rows, block), lambda i: (0, 0, 0, i)),
            pick_spec,
            pick_spec,
        ],
        out_specs=[out_spec, out_spec],
        out_shape=[shape, shape],
        name="pack_rows",
    )(volume, pick_up, pick_dn)


def slab_kernel(
    cuts, bounds, first, last, row_s, col_s, off_up, off_dn, vol_ref, *refs
):
    parts = len(cuts)
    up_refs, dn_refs = refs[:parts], refs[parts : 2 * parts]
    refs = refs[2 * parts :]
    acc_in = None
    if not first:
        acc_in, refs = refs[0], refs[1:]
    out_ref, held_ref, band_ref, acc_ref, sems = refs
    step = pl.program_id(0)
    channels, rows, cols = vol_ref.shape
    k = bounds[0] + step

    @pl.when(step == 0)
    def _():
        copies = []
        start = 0
        for p in range(parts):
            size = cuts[p]
            for d, source in enumerate((up_refs[p], dn_refs[p])):
                target = held_ref.at[pl.ds(d * sum(cuts) + start, size)]
                copies.append(pltpu.make_async_copy(source, target, sems.at[2 * p + d]))
            start += size
        if not first:
            copies.append(pltpu.make_async_copy(acc_in, acc_ref, sems.at[2 * parts]))
        for copy in copies:
            copy.start()
        if first:
            acc_ref[...] = jnp.zeros_like(acc_ref)
        band_ref[...] = jnp.zeros_like(band_ref)
        for copy in copies:
            copy.wait()

    @pl.when(k < bounds[1])
    def _():
        s = row_s[k]
        t = col_s[k]
        chunk = 512
        total = sum(cuts)
        ou = off_up[k]
        od = off_dn[k]
        count = jnp.maximum(0, 1 - s)
        gu = jnp.minimum(ou // GROUP, total - jnp.where(s > 0, 2, 1))
        gd = jnp.minimum(od // GROUP, total - jnp.where(s < 0, 2, 1))
        row_up = rows + gu * GROUP - ou
        row_dn = gd * GROUP - od - count
        g0 = jnp.where(s >= 0, gu, total + gd)
        g1 = jnp.where(s > 0, gu + 1, total + gd + jnp.where(s < 0, 1, 0))
        y = iota((rows, rows), 0)
        r = iota((rows, rows), 1)
        w_own = weight_of(r - y - s)
        y = iota((rows, GROUP), 0)
        q = iota((rows, GROUP), 1)
        r = q + jnp.where(s >= 0, row_up, row_dn)
        kept = jnp.where(s >= 0, r - rows, -1 - r) >= 0
        w_0 = jnp.where(kept, weight_of(r - y - s), 0.0)
        r = q + jnp.where(s > 0, row_up + GROUP, row_dn + jnp.where(s < 0, GROUP, 0))
        kept = jnp.where(s > 0, r - rows, -1 - r) >= 0
        w_1 = jnp.where(kept, weight_of(r - y - s), 0.0)
        w_all = jnp.concatenate([w_own, w_0, w_1], 1).astype(BF)

        @pl.loop(0, cols // chunk, unroll=4)
        def _(j):
            at = pl.multiple_of(j * chunk, chunk)
            here = pl.ds(at, chunk)
            opacity = vol_ref[channels - 1, :, here]
            for c in range(channels):
                own = opacity if c == channels - 1 else vol_ref[c, :, here] * opacity
                data = jnp.concatenate([own, held_ref[g0, c, :, here], held_ref[g1, c, :, here]], 0)
                band = jnp.dot(w_all, data, preferred_element_type=F32)
                band_ref[c * rows : (c + 1) * rows, pl.ds(at + PAD, chunk)] = band.astype(BF)

        block = 256
        shape = (block + 2 * PAD, block)
        w_col = weight_of(iota(shape, 0) - PAD - iota(shape, 1) - t).astype(BF)

        @pl.loop(0, cols // block, unroll=4)
        def _(j):
            at = pl.multiple_of(j * block, block)
            here = pl.ds(at, block)
            sheared = jnp.dot(
                band_ref[:, pl.ds(at, block + 2 * PAD)], w_col, preferred_element_type=F32
            )
            clear = 1.0 - acc_ref[channels - 1, :, here]
            for c in range(channels):
                acc_ref[c, :, here] += clear * sheared[c * rows : (c + 1) * rows, :]

    @pl.when(step == pl.num_programs(0) - 1)
    def _():
        if not last:
            copy = pltpu.make_async_copy(acc_ref, out_ref, sems.at[2 * parts])
            copy.start()
            copy.wait()
            return
        tiles, _, _, wide = out_ref.shape
        tile = wide - 2 * PAD
        edge = jnp.zeros((channels, rows, PAD), BF)
        for i in range(tiles):
            low = i * tile - PAD
            high = (i + 1) * tile + PAD
            if i == 0:
                out_ref[i, :, :, :PAD] = edge
            else:
                out_ref[i, :, :, :PAD] = acc_ref[:, :, low : low + PAD].astype(BF)
            out_ref[i, :, :, PAD : PAD + tile] = acc_ref[:, :, i * tile : (i + 1) * tile].astype(BF)
            if i == tiles - 1:
                out_ref[i, :, :, PAD + tile :] = edge
            else:
                out_ref[i, :, :, PAD + tile :] = acc_ref[:, :, high - PAD : high].astype(BF)


def slab_stage(volume, ups, dns, carry, bounds, scalars, cuts, tiles, last):
    channels, slab, rows, cols = volume.shape
    wide = cols // tiles + 2 * PAD
    parts = len(cuts)
    first = carry is None
    hbm = pl.BlockSpec(memory_space=pl.ANY)
    held = pltpu.VMEM((2 * sum(cuts), channels, GROUP, cols), BF)

    def slice_at(i, bounds_ref, *_):
        return 0, jnp.clip(bounds_ref[0] + i, 0, jnp.maximum(bounds_ref[1] - 1, 0)), 0, 0

    if last:
        out_spec = pl.BlockSpec((tiles, channels, rows, wide), lambda i, *_: (0, 0, 0, 0))
        out_shape = jax.ShapeDtypeStruct((tiles, channels, rows, wide), BF)
    else:
        out_spec = hbm
        out_shape = jax.ShapeDtypeStruct((channels, rows, cols), F32)
    return pl.pallas_call(
        functools.partial(slab_kernel_entry, cuts, first, last),
        grid_spec=pltpu.PrefetchScalarGridSpec(
            num_scalar_prefetch=5,
            grid=(slab,),
            in_specs=[pl.BlockSpec((channels, None, rows, cols), slice_at)]
            + [hbm] * (2 * parts + (0 if first else 1)),
            out_specs=out_spec,
            scratch_shapes=[
                held,
                pltpu.VMEM((channels * rows, cols + 2 * PAD), BF),
                pltpu.VMEM((channels, rows, cols), F32),
                pltpu.SemaphoreType.DMA((2 * parts + 1,)),
            ],
        ),
        out_shape=out_shape,
        compiler_params=pltpu.CompilerParams(vmem_limit_bytes=56 * 2**20),
        cost_estimate=pl.CostEstimate(
            flops=2 * 10**10, bytes_accessed=10**8, transcendentals=0
        ),
        name="slab_stage",
    )(bounds, *scalars, volume, *ups, *dns, *([] if first else [carry]))


def slab_kernel_entry(cuts, first, last, bounds, *refs):
    slab_kernel(cuts, bounds, first, last, *refs)


def cuts_of(count):
    if count < 4:
        return [count]
    small = count // 3
    big = count - 2 * small
    return [big, small, small] if count % 3 != 2 else [small + 1, small + 1, small]


def across_kernel(me_ref, shift_ref, *refs):
    part_refs = refs[:-3]
    out_ref, low_ref, high_ref = refs[-3:]
    count = len(part_refs)
    _, channels, rows, wide = (1,) + part_refs[0].shape
    tile = wide - 2 * PAD
    me = me_ref[0]

    def gather(position):
        result = part_refs[0][...].astype(F32)
        for m in range(1, count):
            result = jnp.where((position ^ me) == m, part_refs[m][...].astype(F32), result)
        return result

    image = gather(0)
    for position in range(1, count):
        image = image + (1.0 - image[channels - 1 : channels]) * gather(position)
    shifts = shift_ref[...]
    for c in range(channels):
        flat = image[c]
        spread = 0.5 * flat + 0.25 * (pltpu.roll(flat, 1, 1) + pltpu.roll(flat, wide - 1, 1))
        moved = jnp.zeros_like(flat)
        for v in range(-SHIFT, SHIFT + 1):
            rolled = spread if v == 0 else pltpu.roll(spread, (-v) % wide, 1)
            moved = jnp.where(shifts == v, rolled, moved)
        across = moved[:, PAD : PAD + tile]
        out_ref[c] = across
        low_ref[c] = across[:GROUP].astype(BF)
        high_ref[c] = across[rows - GROUP :].astype(BF)


def across_image(parts, me, shifts):
    channels, rows, wide = parts[0].shape
    tile = wide - 2 * PAD
    vmem = pl.BlockSpec(memory_space=pltpu.VMEM)
    half = jax.ShapeDtypeStruct((channels, GROUP, tile), BF)
    return pl.pallas_call(
        across_kernel,
        in_specs=[pl.BlockSpec(memory_space=pltpu.SMEM), vmem] + [vmem] * len(parts),
        out_specs=[vmem] * 3,
        out_shape=[jax.ShapeDtypeStruct((channels, rows, tile), F32), half, half],
        name="across_image",
    )(me, shifts, *parts)


def final_kernel(shift_ref, mid_ref, low_ref, high_ref, out_ref, ext_ref):
    channels, rows, tile = mid_ref.shape
    shifts = shift_ref[...]
    for c in range(channels):
        ext_ref[:GROUP] = low_ref[c].astype(F32)
        ext_ref[GROUP : GROUP + rows] = mid_ref[c]
        ext_ref[GROUP + rows :] = high_ref[c].astype(F32)
        moved = jnp.zeros((rows + 2, tile), F32)
        for v in range(-SHIFT, SHIFT + 1):
            start = GROUP + v - 1
            moved = jnp.where(shifts == v, ext_ref[start : start + rows + 2], moved)
        out_ref[c] = 0.5 * moved[1 : rows + 1] + 0.25 * (moved[:rows] + moved[2 : rows + 2])


def final_rows(mid, low, high, shifts):
    channels, rows, tile = mid.shape
    block = 256
    return pl.pallas_call(
        final_kernel,
        grid=(tile // block,),
        in_specs=[
            pl.BlockSpec((1, block), lambda i: (0, i)),
            pl.BlockSpec((channels, rows, block), lambda i: (0, 0, i)),
            pl.BlockSpec((channels, GROUP, block), lambda i: (0, 0, i)),
            pl.BlockSpec((channels, GROUP, block), lambda i: (0, 0, i)),
        ],
        out_specs=pl.BlockSpec((channels, rows, block), lambda i: (0, 0, i)),
        out_shape=jax.ShapeDtypeStruct((channels, rows, tile), F32),
        scratch_shapes=[pltpu.VMEM((rows + 2 * GROUP, block), F32)],
        name="final_rows",
    )(shifts, mid, low, high)


def neighbours(axis):
    count = lax.axis_size(axis)
    forward = [(i, i + 1) for i in range(count - 1)]
    return forward, [(b, a) for a, b in forward]


def swapped(value, axis, mask):
    pairs = [(source, source ^ mask) for source in range(lax.axis_size(axis))]
    return lax.ppermute(value, axis, pairs)


def per_device(volume, shear_rows, shear_cols, warp_cols, warp_rows):
    channels, slab, rows, cols = volume.shape
    depth = lax.axis_size("depth")
    me = lax.axis_index("depth")
    groups = -(-slab * RIM // GROUP)
    forward, backward = neighbours("rows")

    n_up = jnp.maximum(0, shear_rows + 1)
    n_dn = jnp.maximum(0, 1 - shear_rows)
    end_up = jnp.cumsum(n_up)
    end_dn = jnp.cumsum(n_dn)
    off_up = end_up - n_up
    off_dn = end_dn - n_dn
    need = jnp.maximum(end_up[-1], end_dn[-1]).astype(jnp.int32)
    step = 1
    while step < depth:
        need = jnp.maximum(need, swapped(need, "depth", step))
        step *= 2
    row = jnp.arange(GROUP, dtype=jnp.int32)
    at_up = jnp.where(row[None] < n_up[:, None], off_up[:, None] + row[None], -1).reshape(-1)
    back = row[None] - (GROUP - n_dn[:, None])
    at_dn = jnp.where(back >= 0, off_dn[:, None] + back, -1).reshape(-1)
    slot = jnp.arange(groups * GROUP, dtype=jnp.int32)[:, None]
    pick_up = (slot == at_up[None]).astype(BF)
    pick_dn = (slot == at_dn[None]).astype(BF)
    send_up, send_dn = pack(volume, pick_up, pick_dn)

    scalars = (shear_rows, shear_cols, off_up, off_dn)

    def render(count):
        cuts = cuts_of(count)

        def run(a, b):
            ups, dns, carry, start, done = [], [], None, 0, jnp.int32(0)
            for p, size in enumerate(cuts):
                up, dn = a[start : start + size], b[start : start + size]
                if p:
                    ups[-1], dns[-1], up, dn = lax.optimization_barrier((ups[-1], dns[-1], up, dn))
                ups.append(lax.ppermute(up, "rows", backward))
                dns.append(lax.ppermute(dn, "rows", forward))
                start += size
            start = 0
            for p, size in enumerate(cuts):
                start += size
                last = p == len(cuts) - 1
                if last:
                    until = jnp.int32(slab)
                else:
                    ready = (end_up <= start * GROUP) & (end_dn <= start * GROUP)
                    until = jnp.sum(ready.astype(jnp.int32))
                bounds = jnp.stack([done, until])
                carry = slab_stage(
                    volume, ups[: p + 1], dns[: p + 1], carry, bounds, scalars,
                    cuts[: p + 1], depth, last,
                )
                done = until
            return carry

        return run

    sizes = sorted(set(range(max(2, groups // 2), groups // 2 + 3)) | {groups})
    which = sum((need > size * GROUP).astype(jnp.int32) for size in sizes[:-1])
    tiles = lax.switch(which, [render(size) for size in sizes], send_up, send_dn)
    parts = []
    for m in range(depth):
        part = lax.dynamic_index_in_dim(tiles, me ^ m, 0, keepdims=False)
        parts.append(part if m == 0 else swapped(part, "depth", m))
    row_start = lax.axis_index("rows") * rows
    row_shifts = lax.dynamic_slice_in_dim(warp_cols, row_start, rows, 0)
    mid, low, high = across_image(parts, me.reshape(1), row_shifts.reshape(rows, 1))
    below = lax.ppermute(high, "rows", forward)
    above = lax.ppermute(low, "rows", backward)
    return final_rows(mid, below, above, warp_rows.reshape(1, -1))


def solution(mesh):
    return jax.shard_map(
        per_device,
        mesh=mesh,
        in_specs=(P(None, "depth", "rows", None), P("depth"), P("depth"), P(), P("depth")),
        out_specs=P(None, "rows", "depth"),
        check_vma=False,
    )
```

```python
import functools

import jax
import jax.numpy as jnp
from jax import lax
from jax.experimental import pallas as pl
from jax.experimental.pallas import tpu as pltpu
from jax.sharding import PartitionSpec as P

SHIFT = 8
RIM = SHIFT + 1
GROUP = 16
PAD = 128
BF = jnp.bfloat16
F32 = jnp.float32


def weight_of(offset):
    return jnp.where(offset == 0, 0.5, jnp.where(jnp.abs(offset) == 1, 0.25, 0.0)).astype(F32)


def iota(shape, dim):
    return lax.broadcasted_iota(jnp.int32, shape, dim)


def pack_kernel(vol_ref, pick_up_ref, pick_dn_ref, up_ref, dn_ref):
    _, slab, rows, cols = vol_ref.shape
    groups = up_ref.shape[0]
    for pick_ref, out_ref, first in ((pick_up_ref, up_ref, 0), (pick_dn_ref, dn_ref, rows - GROUP)):
        pick = pick_ref[...]
        opacity = None
        for c in (3, 2, 1, 0):
            source = vol_ref[c, :, first : first + GROUP, :].reshape(slab * GROUP, cols)
            got = jnp.dot(pick, source, preferred_element_type=F32)
            if c == 3:
                opacity = got
            else:
                got = got * opacity
            out_ref[:, c, :, :] = got.astype(BF).reshape(groups, GROUP, cols)


def pack(volume, pick_up, pick_dn):
    channels, slab, rows, cols = volume.shape
    count = pick_up.shape[0]
    groups = count // GROUP
    block = 512
    out_spec = pl.BlockSpec((groups, channels, GROUP, block), lambda i: (0, 0, 0, i))
    pick_spec = pl.BlockSpec(pick_up.shape, lambda i: (0, 0))
    shape = jax.ShapeDtypeStruct((groups, channels, GROUP, cols), BF)
    return pl.pallas_call(
        pack_kernel,
        grid=(cols // block,),
        in_specs=[
            pl.BlockSpec((channels, slab, rows, block), lambda i: (0, 0, 0, i)),
            pick_spec,
            pick_spec,
        ],
        out_specs=[out_spec, out_spec],
        out_shape=[shape, shape],
        name="pack_rows",
    )(volume, pick_up, pick_dn)


def slab_kernel(
    cuts, bounds, first, last, row_s, col_s, off_up, off_dn, vol_ref, *refs
):
    parts = len(cuts)
    up_refs, dn_refs = refs[:parts], refs[parts : 2 * parts]
    refs = refs[2 * parts :]
    acc_in = None
    if not first:
        acc_in, refs = refs[0], refs[1:]
    out_ref, held_ref, band_ref, acc_ref, sems = refs
    step = pl.program_id(0)
    channels, rows, cols = vol_ref.shape
    k = bounds[0] + step

    @pl.when(step == 0)
    def _():
        copies = []
        start = 0
        for p in range(parts):
            size = cuts[p]
            for d, source in enumerate((up_refs[p], dn_refs[p])):
                target = held_ref.at[pl.ds(d * sum(cuts) + start, size)]
                copies.append(pltpu.make_async_copy(source, target, sems.at[2 * p + d]))
            start += size
        if not first:
            copies.append(pltpu.make_async_copy(acc_in, acc_ref, sems.at[2 * parts]))
        for copy in copies:
            copy.start()
        if first:
            acc_ref[...] = jnp.zeros_like(acc_ref)
        band_ref[...] = jnp.zeros_like(band_ref)
        for copy in copies:
            copy.wait()

    @pl.when(k < bounds[1])
    def _():
        s = row_s[k]
        t = col_s[k]
        chunk = 512
        total = sum(cuts)
        ou = off_up[k]
        od = off_dn[k]
        count = jnp.maximum(0, 1 - s)
        gu = jnp.minimum(ou // GROUP, total - jnp.where(s > 0, 2, 1))
        gd = jnp.minimum(od // GROUP, total - jnp.where(s < 0, 2, 1))
        row_up = rows + gu * GROUP - ou
        row_dn = gd * GROUP - od - count
        g0 = jnp.where(s >= 0, gu, total + gd)
        g1 = jnp.where(s > 0, gu + 1, total + gd + jnp.where(s < 0, 1, 0))
        y = iota((rows, rows), 0)
        r = iota((rows, rows), 1)
        w_own = weight_of(r - y - s)
        y = iota((rows, GROUP), 0)
        q = iota((rows, GROUP), 1)
        r = q + jnp.where(s >= 0, row_up, row_dn)
        kept = jnp.where(s >= 0, r - rows, -1 - r) >= 0
        w_0 = jnp.where(kept, weight_of(r - y - s), 0.0)
        r = q + jnp.where(s > 0, row_up + GROUP, row_dn + jnp.where(s < 0, GROUP, 0))
        kept = jnp.where(s > 0, r - rows, -1 - r) >= 0
        w_1 = jnp.where(kept, weight_of(r - y - s), 0.0)
        w_all = jnp.concatenate([w_own, w_0, w_1], 1).astype(BF)

        @pl.loop(0, cols // chunk, unroll=8)
        def _(j):
            at = pl.multiple_of(j * chunk, chunk)
            here = pl.ds(at, chunk)
            opacity = vol_ref[channels - 1, :, here]
            for c in range(channels):
                own = opacity if c == channels - 1 else vol_ref[c, :, here] * opacity
                data = jnp.concatenate([own, held_ref[g0, c, :, here], held_ref[g1, c, :, here]], 0)
                band = jnp.dot(w_all, data, preferred_element_type=F32)
                band_ref[c * rows : (c + 1) * rows, pl.ds(at + PAD, chunk)] = band.astype(BF)

        block = 256
        shape = (block + 2 * PAD, block)
        w_col = weight_of(iota(shape, 0) - PAD - iota(shape, 1) - t).astype(BF)

        @pl.loop(0, cols // block, unroll=8)
        def _(j):
            at = pl.multiple_of(j * block, block)
            here = pl.ds(at, block)
            sheared = jnp.dot(
                band_ref[:, pl.ds(at, block + 2 * PAD)], w_col, preferred_element_type=F32
            )
            clear = 1.0 - acc_ref[channels - 1, :, here]
            for c in range(channels):
                acc_ref[c, :, here] += clear * sheared[c * rows : (c + 1) * rows, :]

    @pl.when(step == pl.num_programs(0) - 1)
    def _():
        if not last:
            copy = pltpu.make_async_copy(acc_ref, out_ref, sems.at[2 * parts])
            copy.start()
            copy.wait()
            return
        tiles, _, _, wide = out_ref.shape
        tile = wide - 2 * PAD
        edge = jnp.zeros((channels, rows, PAD), BF)
        for i in range(tiles):
            low = i * tile - PAD
            high = (i + 1) * tile + PAD
            if i == 0:
                out_ref[i, :, :, :PAD] = edge
            else:
                out_ref[i, :, :, :PAD] = acc_ref[:, :, low : low + PAD].astype(BF)
            out_ref[i, :, :, PAD : PAD + tile] = acc_ref[:, :, i * tile : (i + 1) * tile].astype(BF)
            if i == tiles - 1:
                out_ref[i, :, :, PAD + tile :] = edge
            else:
                out_ref[i, :, :, PAD + tile :] = acc_ref[:, :, high - PAD : high].astype(BF)


def slab_stage(volume, ups, dns, carry, bounds, scalars, cuts, tiles, last):
    channels, slab, rows, cols = volume.shape
    wide = cols // tiles + 2 * PAD
    parts = len(cuts)
    first = carry is None
    hbm = pl.BlockSpec(memory_space=pl.ANY)
    held = pltpu.VMEM((2 * sum(cuts), channels, GROUP, cols), BF)

    def slice_at(i, bounds_ref, *_):
        return 0, jnp.clip(bounds_ref[0] + i, 0, jnp.maximum(bounds_ref[1] - 1, 0)), 0, 0

    if last:
        out_spec = pl.BlockSpec((tiles, channels, rows, wide), lambda i, *_: (0, 0, 0, 0))
        out_shape = jax.ShapeDtypeStruct((tiles, channels, rows, wide), BF)
    else:
        out_spec = hbm
        out_shape = jax.ShapeDtypeStruct((channels, rows, cols), F32)
    return pl.pallas_call(
        functools.partial(slab_kernel_entry, cuts, first, last),
        grid_spec=pltpu.PrefetchScalarGridSpec(
            num_scalar_prefetch=5,
            grid=(slab,),
            in_specs=[pl.BlockSpec((channels, None, rows, cols), slice_at)]
            + [hbm] * (2 * parts + (0 if first else 1)),
            out_specs=out_spec,
            scratch_shapes=[
                held,
                pltpu.VMEM((channels * rows, cols + 2 * PAD), BF),
                pltpu.VMEM((channels, rows, cols), F32),
                pltpu.SemaphoreType.DMA((2 * parts + 1,)),
            ],
        ),
        out_shape=out_shape,
        compiler_params=pltpu.CompilerParams(vmem_limit_bytes=56 * 2**20),
        cost_estimate=pl.CostEstimate(
            flops=2 * 10**10, bytes_accessed=10**8, transcendentals=0
        ),
        name="slab_stage",
    )(bounds, *scalars, volume, *ups, *dns, *([] if first else [carry]))


def slab_kernel_entry(cuts, first, last, bounds, *refs):
    slab_kernel(cuts, bounds, first, last, *refs)


def cuts_of(count):
    if count < 4:
        return [count]
    small = count // 3
    big = count - 2 * small
    return [big, small, small] if count % 3 != 2 else [small + 1, small + 1, small]


def across_kernel(me_ref, shift_ref, *refs):
    part_refs = refs[:-3]
    out_ref, low_ref, high_ref = refs[-3:]
    count = len(part_refs)
    _, channels, rows, wide = (1,) + part_refs[0].shape
    tile = wide - 2 * PAD
    me = me_ref[0]

    def gather(position):
        result = part_refs[0][...].astype(F32)
        for m in range(1, count):
            result = jnp.where((position ^ me) == m, part_refs[m][...].astype(F32), result)
        return result

    image = gather(0)
    for position in range(1, count):
        image = image + (1.0 - image[channels - 1 : channels]) * gather(position)
    shifts = shift_ref[...]
    for c in range(channels):
        flat = image[c]
        spread = 0.5 * flat + 0.25 * (pltpu.roll(flat, 1, 1) + pltpu.roll(flat, wide - 1, 1))
        moved = jnp.zeros_like(flat)
        for v in range(-SHIFT, SHIFT + 1):
            rolled = spread if v == 0 else pltpu.roll(spread, (-v) % wide, 1)
            moved = jnp.where(shifts == v, rolled, moved)
        across = moved[:, PAD : PAD + tile]
        out_ref[c] = across
        low_ref[c] = across[:GROUP].astype(BF)
        high_ref[c] = across[rows - GROUP :].astype(BF)


def across_image(parts, me, shifts):
    channels, rows, wide = parts[0].shape
    tile = wide - 2 * PAD
    vmem = pl.BlockSpec(memory_space=pltpu.VMEM)
    half = jax.ShapeDtypeStruct((channels, GROUP, tile), BF)
    return pl.pallas_call(
        across_kernel,
        in_specs=[pl.BlockSpec(memory_space=pltpu.SMEM), vmem] + [vmem] * len(parts),
        out_specs=[vmem] * 3,
        out_shape=[jax.ShapeDtypeStruct((channels, rows, tile), F32), half, half],
        name="across_image",
    )(me, shifts, *parts)


def final_kernel(shift_ref, mid_ref, low_ref, high_ref, out_ref, ext_ref):
    channels, rows, tile = mid_ref.shape
    shifts = shift_ref[...]
    for c in range(channels):
        ext_ref[:GROUP] = low_ref[c].astype(F32)
        ext_ref[GROUP : GROUP + rows] = mid_ref[c]
        ext_ref[GROUP + rows :] = high_ref[c].astype(F32)
        moved = jnp.zeros((rows + 2, tile), F32)
        for v in range(-SHIFT, SHIFT + 1):
            start = GROUP + v - 1
            moved = jnp.where(shifts == v, ext_ref[start : start + rows + 2], moved)
        out_ref[c] = 0.5 * moved[1 : rows + 1] + 0.25 * (moved[:rows] + moved[2 : rows + 2])


def final_rows(mid, low, high, shifts):
    channels, rows, tile = mid.shape
    block = 256
    return pl.pallas_call(
        final_kernel,
        grid=(tile // block,),
        in_specs=[
            pl.BlockSpec((1, block), lambda i: (0, i)),
            pl.BlockSpec((channels, rows, block), lambda i: (0, 0, i)),
            pl.BlockSpec((channels, GROUP, block), lambda i: (0, 0, i)),
            pl.BlockSpec((channels, GROUP, block), lambda i: (0, 0, i)),
        ],
        out_specs=pl.BlockSpec((channels, rows, block), lambda i: (0, 0, i)),
        out_shape=jax.ShapeDtypeStruct((channels, rows, tile), F32),
        scratch_shapes=[pltpu.VMEM((rows + 2 * GROUP, block), F32)],
        name="final_rows",
    )(shifts, mid, low, high)


def neighbours(axis):
    count = lax.axis_size(axis)
    forward = [(i, i + 1) for i in range(count - 1)]
    return forward, [(b, a) for a, b in forward]


def swapped(value, axis, mask):
    pairs = [(source, source ^ mask) for source in range(lax.axis_size(axis))]
    return lax.ppermute(value, axis, pairs)


def per_device(volume, shear_rows, shear_cols, warp_cols, warp_rows):
    channels, slab, rows, cols = volume.shape
    depth = lax.axis_size("depth")
    me = lax.axis_index("depth")
    groups = -(-slab * RIM // GROUP)
    forward, backward = neighbours("rows")

    n_up = jnp.maximum(0, shear_rows + 1)
    n_dn = jnp.maximum(0, 1 - shear_rows)
    end_up = jnp.cumsum(n_up)
    end_dn = jnp.cumsum(n_dn)
    off_up = end_up - n_up
    off_dn = end_dn - n_dn
    need = jnp.maximum(end_up[-1], end_dn[-1]).astype(jnp.int32)
    step = 1
    while step < depth:
        need = jnp.maximum(need, swapped(need, "depth", step))
        step *= 2
    row = jnp.arange(GROUP, dtype=jnp.int32)
    at_up = jnp.where(row[None] < n_up[:, None], off_up[:, None] + row[None], -1).reshape(-1)
    back = row[None] - (GROUP - n_dn[:, None])
    at_dn = jnp.where(back >= 0, off_dn[:, None] + back, -1).reshape(-1)
    slot = jnp.arange(groups * GROUP, dtype=jnp.int32)[:, None]
    pick_up = (slot == at_up[None]).astype(BF)
    pick_dn = (slot == at_dn[None]).astype(BF)
    send_up, send_dn = pack(volume, pick_up, pick_dn)

    scalars = (shear_rows, shear_cols, off_up, off_dn)

    def render(count):
        cuts = cuts_of(count)

        def run(a, b):
            ups, dns, carry, start, done = [], [], None, 0, jnp.int32(0)
            for p, size in enumerate(cuts):
                up, dn = a[start : start + size], b[start : start + size]
                if p:
                    ups[-1], up = lax.optimization_barrier((ups[-1], up))
                    dns[-1], dn = lax.optimization_barrier((dns[-1], dn))
                ups.append(lax.ppermute(up, "rows", backward))
                dns.append(lax.ppermute(dn, "rows", forward))
                start += size
            start = 0
            for p, size in enumerate(cuts):
                start += size
                last = p == len(cuts) - 1
                if last:
                    until = jnp.int32(slab)
                else:
                    ready = (end_up <= start * GROUP) & (end_dn <= start * GROUP)
                    until = jnp.sum(ready.astype(jnp.int32))
                bounds = jnp.stack([done, until])
                carry = slab_stage(
                    volume, ups[: p + 1], dns[: p + 1], carry, bounds, scalars,
                    cuts[: p + 1], depth, last,
                )
                done = until
            return carry

        return run

    sizes = sorted(set(range(max(2, groups // 2), groups // 2 + 3)) | {groups})
    which = sum((need > size * GROUP).astype(jnp.int32) for size in sizes[:-1])
    tiles = lax.switch(which, [render(size) for size in sizes], send_up, send_dn)
    parts = []
    for m in range(depth):
        part = lax.dynamic_index_in_dim(tiles, me ^ m, 0, keepdims=False)
        parts.append(part if m == 0 else swapped(part, "depth", m))
    row_start = lax.axis_index("rows") * rows
    row_shifts = lax.dynamic_slice_in_dim(warp_cols, row_start, rows, 0)
    mid, low, high = across_image(parts, me.reshape(1), row_shifts.reshape(rows, 1))
    below = lax.ppermute(high, "rows", forward)
    above = lax.ppermute(low, "rows", backward)
    return final_rows(mid, below, above, warp_rows.reshape(1, -1))


def solution(mesh):
    return jax.shard_map(
        per_device,
        mesh=mesh,
        in_specs=(P(None, "depth", "rows", None), P("depth"), P("depth"), P(), P("depth")),
        out_specs=P(None, "rows", "depth"),
        check_vma=False,
    )
```
